32 devices in a mesh: trial: 8 (over z, y), tensor: 4 (over x, core).
Axes of the slice: x: 2, y: 2, z: 4, core: 2. Of those that a mesh axis runs over, the one named last changes fastest.
Arguments:
- stored_attention: bfloat16 [8, 1024, 8192], P('trial', None, 'tensor'), may hold values from -6 to 6
- output_gradient: bfloat16 [8, 1024, 8192], P('trial', 'tensor'), may hold values from -6 to 6
- output_weight: bfloat16 [8192, 8192], P('tensor', 'trial'), may hold values from -0.0625 to 0.0625
- down_adapter: bfloat16 [8, 8192, 128], P('trial', 'tensor'), may hold values from -0.0625 to 0.0625
- up_adapter: bfloat16 [8, 128, 8192], P('trial'), may hold values from -0.0625 to 0.0625
- lengths: int32 [8], P('trial'), may hold values from 128 to 1024, as said below
- ranks: int32 [8], P('trial'), may hold values from 16 to 128, as said below
Outputs:
- attention_gradient: bfloat16 [8, 1024, 8192], P('trial', None, 'tensor')
- down_gradient: float32 [8, 8192, 128], P('trial', 'tensor')
- up_gradient: float32 [8, 128, 8192], P('trial', None, 'tensor')
The draws below stay inside these ranges and needn't reach their ends.
Inputs may be any that keep to these rules, and one draw needn't show every extreme that they name: `lengths`: rows at or beyond a trial's count are padding; some trial has all 1024 rows live. `ranks`: each rank is a multiple of 16; some trial has rank 128 and some has 16.
All inputs are finite; a program needn't handle non-finite values.
Results may differ from the reference program's by a relative error of at most 0.0034.
Values may be sent and summed in bfloat16 or wider, within the bound.
A program may use at most 128 MiB of HBM per device.

```python
from functools import partial
import jax
import jax.numpy as jnp
from jax import lax

MODEL_WIDTH = 8192
MAX_RANK = 128
TOK = 1024
TRIAL_COUNT = 8


def draw_lengths(key, part):
    first_key, second_key = jax.random.split(jax.random.fold_in(key, 11))
    values_drawn = jax.random.randint(first_key, (TRIAL_COUNT,), TOK // 8, TOK + 1)
    full_trial = jax.random.randint(second_key, (), 0, TRIAL_COUNT)
    return jnp.where(jnp.arange(TRIAL_COUNT) == full_trial, TOK, values_drawn).astype(jnp.int32)


def draw_ranks(key, part):
    first_key, second_key = jax.random.split(jax.random.fold_in(key, 23))
    values_drawn = MAX_RANK // 8 * jax.random.randint(first_key, (TRIAL_COUNT,), 1, 9)
    chosen = jax.random.permutation(second_key, TRIAL_COUNT)
    values_drawn = jnp.where(jnp.arange(TRIAL_COUNT) == chosen[0], MAX_RANK, values_drawn)
    values_drawn = jnp.where(jnp.arange(TRIAL_COUNT) == chosen[1], MAX_RANK // 8, values_drawn)
    return values_drawn.astype(jnp.int32)


def levels(rng, extent, shards, low, high):
    def one(dim, blocks):
        steps = jax.random.uniform(jax.random.fold_in(jax.random.fold_in(rng, 6), dim), (blocks,), jnp.float32, low / len(shards), high / len(shards))
        return jnp.repeat(jnp.exp(steps), extent[dim] // blocks).reshape((-1,) + (1,) * (len(extent) - dim - 1))

    loudness = one(*shards[0])
    for cut in shards[1:]:
        loudness = loudness * one(*cut)
    return loudness


def gaussian(own_key, dims, spread, limit, pieces=(), kind=jnp.bfloat16):
    entries = spread * jax.random.normal(own_key, dims, jnp.float32)
    if pieces:
        entries = entries * levels(own_key, dims, pieces, -0.22, 0.18)
    return jnp.clip(entries, -limit, limit).astype(kind)


def setup_inputs(seed: int = 0) -> dict:
    splits = jax.random.split(jax.random.key(seed), 8)
    return {
        "stored_attention": gaussian(splits[0], (TRIAL_COUNT, TOK, MODEL_WIDTH), 1.0, 6.0, ((0, 8), (2, 4))),
        "output_gradient": gaussian(splits[1], (TRIAL_COUNT, TOK, MODEL_WIDTH), 1.0, 6.0, ((0, 8), (1, 4))),
        "output_weight": gaussian(splits[2], (MODEL_WIDTH, MODEL_WIDTH), MODEL_WIDTH ** -0.5, 0.0625, ((0, 4), (1, 8))),
        "down_adapter": gaussian(splits[3], (TRIAL_COUNT, MODEL_WIDTH, MAX_RANK), MODEL_WIDTH ** -0.5, 0.0625, ((0, 8), (1, 4))),
        "up_adapter": gaussian(splits[4], (TRIAL_COUNT, MAX_RANK, MODEL_WIDTH), MODEL_WIDTH ** -0.5, 0.0625, ((0, 8),)),
        "lengths": draw_lengths(jax.random.fold_in(splits[7], 71), 0),
        "ranks": draw_ranks(jax.random.fold_in(splits[7], 71), 0),
    }


adapter_alpha = 32.0

def single_trial(output_weight, inputs):
    attention_rows, gradient_rows, a_mat, b_mat, length, adapter_rank = inputs
    rank_mask = jnp.arange(a_mat.shape[1]) < adapter_rank
    adapter_scale = adapter_alpha / jnp.sqrt(adapter_rank.astype(jnp.float32))
    a_low = jnp.where(rank_mask[None, :], a_mat, jnp.zeros_like(a_mat))
    b_low = jnp.where(rank_mask[:, None], b_mat, jnp.zeros_like(b_mat))
    live_rows = jnp.arange(gradient_rows.shape[0]) < length
    gradient_rows = jnp.where(live_rows[:, None], gradient_rows, jnp.zeros_like(gradient_rows))
    lowrank_left = jnp.dot(gradient_rows, b_low.T, preferred_element_type=jnp.float32).astype(jnp.bfloat16)
    lowrank_right = jnp.dot(attention_rows, a_low, preferred_element_type=jnp.float32).astype(jnp.bfloat16)
    dense_piece = jnp.dot(gradient_rows, output_weight.T, preferred_element_type=jnp.float32)
    lowrank_piece = jnp.dot(lowrank_left, a_low.T, preferred_element_type=jnp.float32)
    attention_gradient = (dense_piece + adapter_scale * lowrank_piece).astype(jnp.bfloat16)
    count_of_rows = float(gradient_rows.shape[0])
    down_gradient = adapter_scale * jnp.dot(attention_rows.T, lowrank_left, preferred_element_type=jnp.float32) / count_of_rows
    up_gradient = adapter_scale * jnp.dot(lowrank_right.T, gradient_rows, preferred_element_type=jnp.float32) / count_of_rows
    return (attention_gradient, down_gradient, up_gradient)

def reference(stored_attention, output_gradient, output_weight, down_adapter, up_adapter, lengths, ranks):
    trial_results = lax.map(partial(single_trial, output_weight), (stored_attention, output_gradient, down_adapter, up_adapter, lengths, ranks))
    return (trial_results[0], trial_results[1], trial_results[2])
```

```python
import functools

import jax
import jax.numpy as jnp
from jax import lax
from jax.experimental import pallas as pl
from jax.experimental.pallas import tpu as pltpu
from jax.sharding import PartitionSpec as P

adapter_alpha = 32.0
MESH = pl.DeviceIdType.MESH
NT = (((1,), (1,)), ((), ()))


def row_product(left, right):
    return jnp.einsum("tk,hk->th", left, right, preferred_element_type=jnp.float32)


def dense_kernel(
    planes, chunks, wide,
    dy_ref, w_ref, dense_ref, dyup_ref,
    wv, dyv, part, prec, acc,
    w_loc, w_up, w_dn, w_recv,
    dy_loc, dyy_send, dyx_send, dyc_send, dy_recv,
    p_send, p_recv, o_sem, up_sem,
):
    trial, s = lax.axis_index("trial"), lax.axis_index("tensor")
    z, y = trial // 2, trial % 2
    x, c = s // 2, s % 2
    oy = 1 - y
    s_c, s_x, s_xc = 2 * x + 1 - c, 2 * (1 - x) + c, 2 * (1 - x) + 1 - c
    rows, width = dy_ref.shape[0], w_ref.shape[1]
    tokens = dyv.shape[2]
    head = chunks // 2
    to_core, to_x, to_y = (trial, s_c), (trial, s_x), (2 * z + oy, s)
    above, below = z < planes - 1, z > 0
    inner = jnp.logical_and(above, below)

    def copy(src, dst, ss, rs, dev):
        return pltpu.make_async_remote_copy(
            src_ref=src, dst_ref=dst, send_sem=ss, recv_sem=rs,
            device_id=dev, device_id_type=MESH)

    def w_slot(zz, n):
        return wv.at[zz, pl.ds(pl.multiple_of(n * wide, wide), wide), :]

    def w_own(n):
        return w_ref.at[pl.ds(pl.multiple_of(n * wide, wide), wide), :]

    def w_send(zz, n, up, own):
        src = w_own(n) if own else w_slot(zz, n)
        sem = w_up if up else w_dn
        dev = (trial + 2, s) if up else (trial - 2, s)
        return copy(src, w_slot(zz, n), sem.at[zz, n], w_recv.at[zz, n], dev)

    def w_arrived(zz, n):
        copy(w_slot(zz, n), w_slot(zz, n), w_up.at[zz, n], w_recv.at[zz, n], to_y).wait_recv()

    def start_own(n):
        @pl.when(above)
        def _():
            w_send(z, n, True, True).start()

        @pl.when(below)
        def _():
            w_send(z, n, False, True).start()

    def forward(hop, n):
        @pl.when(jnp.logical_and(inner, z + hop < planes))
        def _():
            w_arrived(z + hop, n)
            w_send(z + hop, n, False, False).start()

        @pl.when(jnp.logical_and(inner, z - hop >= 0))
        def _():
            w_arrived(z - hop, n)
            w_send(z - hop, n, True, False).start()

    def dy_own(j, parity):
        start = pl.multiple_of((2 * j + parity) * width, width)
        return dy_ref.at[:, pl.ds(start, width)]

    def dy_slot(yy, ss, j):
        return dyv.at[yy, j, pl.ds(pl.multiple_of(ss * rows, rows), rows), :]

    def dy_send(src, yy, ss, j, sem, dev):
        return copy(src, dy_slot(yy, ss, j), sem, dy_recv.at[yy, ss, j], dev)

    def dy_arrived(yy, ss, j):
        slot = dy_slot(yy, ss, j)
        dy_send(slot, yy, ss, j, dyy_send.at[j], to_y).wait_recv()

    def first_copies(j):
        return (
            dy_send(dy_own(j, oy), y, s, j, dyy_send.at[j], to_y),
            dy_send(dy_own(j, y), y, s, j, dyx_send.at[0, j], to_x),
            dy_send(dy_own(j, y), y, s, j, dyc_send.at[0, j], to_core),
        )

    def local_dy(j):
        return pltpu.make_async_copy(dy_own(j, y), dy_slot(y, s, j), dy_loc.at[j])

    def local_w(n):
        return pltpu.make_async_copy(w_own(n), w_slot(z, n), w_loc.at[n])

    def later_copies(j):
        return (
            dy_send(dy_slot(oy, s, j), oy, s, j, dyx_send.at[1, j], to_x),
            dy_send(dy_slot(oy, s, j), oy, s, j, dyc_send.at[1, j], to_core),
            dy_send(dy_slot(y, s_x, j), y, s_x, j, dyc_send.at[2, j], to_core),
            dy_send(dy_slot(oy, s_x, j), oy, s_x, j, dyc_send.at[3, j], to_core),
        )

    def partial_copy(n):
        return copy(part.at[n], prec.at[n], p_send.at[n], p_recv.at[n], to_y)

    def out_copy(n):
        cols = pl.ds(pl.multiple_of(n * wide, wide), wide)
        return pltpu.make_async_copy(acc.at[n % 2], dense_ref.at[:, cols], o_sem.at[n % 2])

    def loop(lo, hi, fn):
        def step(i, carry):
            fn(i)
            return carry
        lax.fori_loop(lo, hi, step, 0)

    barrier = pltpu.get_barrier_semaphore()
    for dev in (to_core, to_x, to_y):
        pl.semaphore_signal(barrier, inc=1, device_id=dev, device_id_type=MESH)

    @pl.when(above)
    def _():
        pl.semaphore_signal(barrier, inc=1, device_id=(trial + 2, s), device_id_type=MESH)

    @pl.when(below)
    def _():
        pl.semaphore_signal(barrier, inc=1, device_id=(trial - 2, s), device_id_type=MESH)

    @pl.when(inner)
    def _():
        pl.semaphore_wait(barrier, 5)

    @pl.when(jnp.logical_not(inner))
    def _():
        pl.semaphore_wait(barrier, 4)

    loop(0, head, start_own)

    def begin(j):
        for item in first_copies(j):
            item.start()
        local_dy(j).start()
    loop(0, planes, begin)
    loop(0, chunks, lambda n: local_w(n).start())

    def spread(j):
        over_x, over_core, from_x, _ = later_copies(j)
        dy_arrived(oy, s, j)
        over_x.start()
        over_core.start()
        dy_arrived(y, s_x, j)
        from_x.start()
        forward(1, j)
    loop(0, planes, spread)
    loop(planes, head, lambda n: forward(1, n))

    def spread_far(j):
        dy_arrived(oy, s_x, j)
        later_copies(j)[3].start()
        for hop in range(2, planes - 1):
            forward(hop, j)
        start_own(head + j)
    loop(0, planes, spread_far)

    def rest(n):
        for hop in range(2, planes - 1):
            forward(hop, n)
        start_own(head + n)
    loop(planes, head, rest)

    def settle(j):
        local_dy(j).wait()
        for yy in (y, oy):
            dy_arrived(yy, s_c, j)
            dy_arrived(yy, s_xc, j)
    loop(0, planes, settle)
    dyup = pltpu.make_async_copy(dyv.at[:, s], dyup_ref, up_sem)
    dyup.start()

    block = min(512, tokens)

    def product(yy, n, i):
        start = pl.multiple_of(i * block, block)
        total = None
        for j in range(planes):
            piece = lax.dot_general(
                dyv[yy, j, pl.ds(start, block), :],
                wv[j, pl.ds(pl.multiple_of(n * wide, wide), wide), :],
                NT, preferred_element_type=jnp.float32)
            total = piece if total is None else total + piece
        return total, pl.ds(start, block)

    def finish(n):
        partial_copy(n).wait_recv()

        def add(i):
            at = pl.ds(pl.multiple_of(i * block, block), block)
            acc[n % 2, at, :] = acc[n % 2, at, :] + prec[n, at, :].astype(jnp.float32)
        loop(0, tokens // block, add)
        out_copy(n).start()

    def compute(n):
        local_w(n).wait()

        @pl.when(jnp.logical_not(inner))
        def _():
            for hop in range(1, planes):
                @pl.when(z + hop < planes)
                def _():
                    w_arrived(z + hop, n)

                @pl.when(z - hop >= 0)
                def _():
                    w_arrived(z - hop, n)

        def other(i):
            value, at = product(oy, n, i)
            part[n, at, :] = value.astype(part.dtype)
        loop(0, tokens // block, other)
        partial_copy(n).start()

        @pl.when(n >= 2)
        def _():
            out_copy(n - 2).wait()

        def own(i):
            value, at = product(y, n, i)
            acc[n % 2, at, :] = value
        loop(0, tokens // block, own)

        @pl.when(n >= 1)
        def _():
            finish(n - 1)

    def early(n):
        forward(1, head + n)
        compute(n)
    loop(0, head, early)

    def late(n):
        for hop in range(2, planes - 1):
            forward(hop, n)
    loop(head, chunks, late)
    loop(head, chunks, compute)
    finish(chunks - 1)

    out_copy(chunks - 2).wait()
    out_copy(chunks - 1).wait()
    dyup.wait()

    def drain_dy(j):
        for item in first_copies(j) + later_copies(j):
            item.wait_send()
    loop(0, planes, drain_dy)

    def drain(n):
        partial_copy(n).wait_send()

        @pl.when(above)
        def _():
            w_send(z, n, True, True).wait_send()

        @pl.when(below)
        def _():
            w_send(z, n, False, True).wait_send()

        for hop in range(1, planes - 1):
            @pl.when(jnp.logical_and(inner, z + hop < planes))
            def _():
                w_send(z + hop, n, False, False).wait_send()

            @pl.when(jnp.logical_and(inner, z - hop >= 0))
            def _():
                w_send(z - hop, n, True, False).wait_send()
    loop(0, chunks, drain)


def dense_exchange(planes, gradient_rows, weight):
    rows, width = gradient_rows.shape[0], weight.shape[1]
    tokens, heads = rows * 4, weight.shape[0]
    wide = min(256, heads // 8)
    chunks = heads // wide
    dma = pltpu.SemaphoreType.DMA
    bf16, f32 = jnp.bfloat16, jnp.float32
    return pl.pallas_call(
        functools.partial(dense_kernel, planes, chunks, wide),
        out_shape=(
            jax.ShapeDtypeStruct((tokens, heads), f32),
            jax.ShapeDtypeStruct((2, tokens, width), bf16),
        ),
        in_specs=[pl.BlockSpec(memory_space=pl.ANY)] * 2,
        out_specs=[pl.BlockSpec(memory_space=pl.ANY)] * 2,
        scratch_shapes=[
            pltpu.VMEM((planes, heads, width), bf16),
            pltpu.VMEM((2, planes, tokens, width), bf16),
            pltpu.VMEM((chunks, tokens, wide), bf16),
            pltpu.VMEM((chunks, tokens, wide), bf16),
            pltpu.VMEM((2, tokens, wide), f32),
            dma((chunks,)), dma((planes, chunks)), dma((planes, chunks)), dma((planes, chunks)),
            dma((planes,)), dma((planes,)), dma((2, planes)), dma((4, planes)), dma((2, 4, planes)),
            dma((chunks,)), dma((chunks,)), dma((2,)), dma,
        ],
        compiler_params=pltpu.CompilerParams(
            collective_id=0, has_side_effects=True, vmem_limit_bytes=60 * 2**20),
        cost_estimate=pl.CostEstimate(
            flops=4 * tokens * heads * planes * width, bytes_accessed=2**27, transcendentals=0),
    )(gradient_rows, weight)


def line_body(
    planes, stored_attention, output_gradient, output_weight, down_adapter, up_adapter, lengths, ranks
):
    attention_rows = stored_attention[0]
    gradient_rows = output_gradient[0]
    down_piece = down_adapter[0]
    up_complete = up_adapter[0]
    adapter_rank = ranks[0]
    token_rows = attention_rows.shape[0]
    y = lax.axis_index("trial") % 2
    rank_mask = jnp.arange(up_complete.shape[0]) < adapter_rank
    adapter_scale = adapter_alpha / jnp.sqrt(adapter_rank.astype(jnp.float32))
    a_low = jnp.where(rank_mask[None, :], down_piece, jnp.zeros_like(down_piece))
    b_low = jnp.where(rank_mask[:, None], up_complete, jnp.zeros_like(up_complete))
    live = (jnp.arange(token_rows) < lengths[0])[:, None]
    u_part = jnp.einsum(
        "td,rd->tr", gradient_rows, b_low, preferred_element_type=jnp.float32
    ).astype(jnp.bfloat16)
    v_partial = jnp.dot(attention_rows, a_low, preferred_element_type=jnp.float32)
    v_all = lax.psum(v_partial, "tensor").astype(jnp.bfloat16)
    u_all = lax.all_gather(u_part, "tensor", axis=0, tiled=True)

    dense, dy_cols = dense_exchange(planes, gradient_rows, output_weight)

    u_all = jnp.where(live, u_all, jnp.zeros_like(u_all))
    v_all = jnp.where(live, v_all, jnp.zeros_like(v_all))
    pairs = [(2 * k + i, 2 * k + 1 - i) for k in range(planes) for i in range(2)]
    v_other = lax.ppermute(v_all, "trial", pairs)
    dy_mine = jnp.where(y == 0, dy_cols[0], dy_cols[1])
    dy_other = jnp.where(y == 0, dy_cols[1], dy_cols[0])
    up_given = jnp.einsum("tr,th->rh", v_other, dy_other, preferred_element_type=jnp.float32)
    up_taken = lax.ppermute(up_given, "trial", pairs)
    up_mine = jnp.einsum("tr,th->rh", v_all, dy_mine, preferred_element_type=jnp.float32)

    lowrank_piece = jnp.einsum("tr,hr->th", u_all, a_low, preferred_element_type=jnp.float32)
    attention_gradient = jnp.where(live, dense + adapter_scale * lowrank_piece, 0.0).astype(jnp.bfloat16)
    down_total = jnp.einsum("th,tr->hr", attention_rows, u_all, preferred_element_type=jnp.float32)
    up_total = jnp.concatenate(
        [jnp.where(y == 0, up_mine, up_taken), jnp.where(y == 0, up_taken, up_mine)], axis=1)
    down_gradient = adapter_scale * down_total / float(token_rows)
    up_gradient = adapter_scale * up_total / float(token_rows)
    return (attention_gradient[None], down_gradient[None], up_gradient[None])


def body(
    stored_attention, output_gradient, output_weight, down_adapter, up_adapter, lengths, ranks
):
    attention_rows = stored_attention[0]
    gradient_rows = output_gradient[0]
    down_piece = down_adapter[0]
    up_complete = up_adapter[0]
    length = lengths[0]
    adapter_rank = ranks[0]
    token_rows = attention_rows.shape[0]
    head_cols = attention_rows.shape[1]
    shard_rows = gradient_rows.shape[0]
    rank_mask = jnp.arange(up_complete.shape[0]) < adapter_rank
    adapter_scale = adapter_alpha / jnp.sqrt(adapter_rank.astype(jnp.float32))
    a_low = jnp.where(rank_mask[None, :], down_piece, jnp.zeros_like(down_piece))
    b_low = jnp.where(rank_mask[:, None], up_complete, jnp.zeros_like(up_complete))
    row_offset = lax.axis_index("tensor") * shard_rows
    live_rows = row_offset + jnp.arange(shard_rows) < length
    gradient_rows = jnp.where(live_rows[:, None], gradient_rows, jnp.zeros_like(gradient_rows))
    u_part = jnp.einsum(
        "td,rd->tr", gradient_rows, b_low, preferred_element_type=jnp.float32
    ).astype(jnp.bfloat16)
    v_partial = jnp.dot(attention_rows, a_low, preferred_element_type=jnp.float32)
    lowrank_right = lax.psum(v_partial, "tensor").astype(jnp.bfloat16)
    col_start = lax.axis_index("tensor") * head_cols
    rows_all, u_all = (
        lax.all_gather(gradient_rows, "tensor", axis=0, tiled=True),
        lax.all_gather(u_part, "tensor", axis=0, tiled=True),
    )
    dense_piece = row_product(rows_all, lax.all_gather(output_weight, "trial", axis=1, tiled=True))
    lowrank_piece = jnp.einsum("tr,hr->th", u_all, a_low, preferred_element_type=jnp.float32)
    attention_gradient = (dense_piece + adapter_scale * lowrank_piece).astype(jnp.bfloat16)
    down_total = jnp.einsum("th,tr->hr", attention_rows, u_all, preferred_element_type=jnp.float32)
    own_cols = lax.dynamic_slice_in_dim(rows_all, col_start, head_cols, 1)
    up_total = jnp.einsum("tr,th->rh", lowrank_right, own_cols, preferred_element_type=jnp.float32)
    down_gradient = adapter_scale * down_total / float(token_rows)
    up_gradient = adapter_scale * up_total / float(token_rows)
    return (attention_gradient[None], down_gradient[None], up_gradient[None])


def solution(mesh):
    placed = (
        P("trial", None, "tensor"),
        P("trial", "tensor", None),
        P("tensor", "trial"),
        P("trial", "tensor", None),
        P("trial", None, None),
        P("trial"),
        P("trial"),
    )
    trials, tensors = mesh.shape["trial"], mesh.shape["tensor"]
    if tensors == 4 and trials == 2 * tensors:
        run = functools.partial(line_body, trials // 2)
    else:
        run = body
    return jax.shard_map(
        run,
        mesh=mesh,
        in_specs=placed,
        out_specs=(
            P("trial", None, "tensor"),
            P("trial", "tensor", None),
            P("trial", None, "tensor"),
        ),
        check_vma=False,
    )
```

```python
import functools

import jax
import jax.numpy as jnp
from jax import lax
from jax.experimental import pallas as pl
from jax.experimental.pallas import tpu as pltpu
from jax.sharding import PartitionSpec as P

adapter_alpha = 32.0
MESH = pl.DeviceIdType.MESH
NT = (((1,), (1,)), ((), ()))


def row_product(left, right):
    return jnp.einsum("tk,hk->th", left, right, preferred_element_type=jnp.float32)


def dense_kernel(
    planes, chunks, wide,
    dy_ref, w_ref, u_ref, v_ref, dense_ref, uall_ref, up_ref,
    wv, dyv, part, prec, acc, uv, vparts, vsum, upv, upg,
    w_loc, w_up, w_dn, w_recv,
    dy_loc, dyy_send, dyx_send, dyc_send, dy_recv,
    p_send, p_recv, o_sem, up_sem,
    low_loc, low_send, u_recv, v_recv, pair_send, pair_recv,
):
    trial, s = lax.axis_index("trial"), lax.axis_index("tensor")
    z, y = trial // 2, trial % 2
    x, c = s // 2, s % 2
    oy = 1 - y
    s_c, s_x, s_xc = 2 * x + 1 - c, 2 * (1 - x) + c, 2 * (1 - x) + 1 - c
    rows, width = dy_ref.shape[0], w_ref.shape[1]
    tokens = dyv.shape[2]
    head = chunks // 2
    to_core, to_x, to_y = (trial, s_c), (trial, s_x), (2 * z + oy, s)
    to_xc = (trial, s_xc)
    above, below = z < planes - 1, z > 0
    inner = jnp.logical_and(above, below)

    def copy(src, dst, ss, rs, dev):
        return pltpu.make_async_remote_copy(
            src_ref=src, dst_ref=dst, send_sem=ss, recv_sem=rs,
            device_id=dev, device_id_type=MESH)

    def w_slot(zz, n):
        return wv.at[zz, pl.ds(pl.multiple_of(n * wide, wide), wide), :]

    def w_own(n):
        return w_ref.at[pl.ds(pl.multiple_of(n * wide, wide), wide), :]

    def w_send(zz, n, up, own):
        src = w_own(n) if own else w_slot(zz, n)
        sem = w_up if up else w_dn
        dev = (trial + 2, s) if up else (trial - 2, s)
        return copy(src, w_slot(zz, n), sem.at[zz, n], w_recv.at[zz, n], dev)

    def w_arrived(zz, n):
        copy(w_slot(zz, n), w_slot(zz, n), w_up.at[zz, n], w_recv.at[zz, n], to_y).wait_recv()

    def start_own(n):
        @pl.when(above)
        def _():
            w_send(z, n, True, True).start()

        @pl.when(below)
        def _():
            w_send(z, n, False, True).start()

    def forward(hop, n):
        @pl.when(jnp.logical_and(inner, z + hop < planes))
        def _():
            w_arrived(z + hop, n)
            w_send(z + hop, n, False, False).start()

        @pl.when(jnp.logical_and(inner, z - hop >= 0))
        def _():
            w_arrived(z - hop, n)
            w_send(z - hop, n, True, False).start()

    def dy_own(j, parity):
        start = pl.multiple_of((2 * j + parity) * width, width)
        return dy_ref.at[:, pl.ds(start, width)]

    def dy_slot(yy, ss, j):
        return dyv.at[yy, j, pl.ds(pl.multiple_of(ss * rows, rows), rows), :]

    def dy_send(src, yy, ss, j, sem, dev):
        return copy(src, dy_slot(yy, ss, j), sem, dy_recv.at[yy, ss, j], dev)

    def dy_arrived(yy, ss, j):
        slot = dy_slot(yy, ss, j)
        dy_send(slot, yy, ss, j, dyy_send.at[j], to_y).wait_recv()

    def first_copies(j):
        return (
            dy_send(dy_own(j, oy), y, s, j, dyy_send.at[j], to_y),
            dy_send(dy_own(j, y), y, s, j, dyx_send.at[0, j], to_x),
            dy_send(dy_own(j, y), y, s, j, dyc_send.at[0, j], to_core),
        )

    def local_dy(j):
        return pltpu.make_async_copy(dy_own(j, y), dy_slot(y, s, j), dy_loc.at[j])

    def local_w(n):
        return pltpu.make_async_copy(w_own(n), w_slot(z, n), w_loc.at[n])

    def later_copies(j):
        return (
            dy_send(dy_slot(oy, s, j), oy, s, j, dyx_send.at[1, j], to_x),
            dy_send(dy_slot(oy, s, j), oy, s, j, dyc_send.at[1, j], to_core),
            dy_send(dy_slot(y, s_x, j), y, s_x, j, dyc_send.at[2, j], to_core),
            dy_send(dy_slot(oy, s_x, j), oy, s_x, j, dyc_send.at[3, j], to_core),
        )

    def partial_copy(n):
        return copy(part.at[n], prec.at[n], p_send.at[n], p_recv.at[n], to_y)

    def out_copy(n):
        cols = pl.ds(pl.multiple_of(n * wide, wide), wide)
        return pltpu.make_async_copy(acc.at[n % 2], dense_ref.at[:, cols], o_sem.at[n % 2])

    def u_slot(ss):
        return uv.at[pl.ds(pl.multiple_of(ss * rows, rows), rows), :]

    peers = ((to_core, s_c), (to_x, s_x), (to_xc, s_xc))

    def low_copies():
        return [
            copy(src, dst, low_send.at[i, k], sem.at[s], dev)
            for k, (dev, _) in enumerate(peers)
            for i, (src, dst, sem) in enumerate(
                ((u_ref, u_slot(s), u_recv), (v_ref, vparts.at[s], v_recv)))
        ]

    def low_local():
        return (
            pltpu.make_async_copy(u_ref, u_slot(s), low_loc.at[0]),
            pltpu.make_async_copy(v_ref, vparts.at[s], low_loc.at[1]),
        )

    def low_settle():
        for item in low_local():
            item.wait()
        for k, (dev, ss) in enumerate(peers):
            copy(u_slot(ss), u_slot(ss), low_send.at[0, k], u_recv.at[ss], dev).wait_recv()
            copy(vparts.at[ss], vparts.at[ss], low_send.at[1, k], v_recv.at[ss], dev).wait_recv()

    def v_copy():
        return copy(vsum.at[y], vsum.at[y], pair_send.at[0], pair_recv.at[0], to_y)

    def up_copy():
        return copy(upg, upv.at[y], pair_send.at[1], pair_recv.at[1], to_y)

    def up_product(yy, put):
        step = min(256, width)
        for i in range(width // step):
            at = pl.ds(i * step, step)
            put(at, jnp.dot(vsum[yy], dyv[yy, s, :, at], preferred_element_type=jnp.float32))

    def loop(lo, hi, fn):
        def step(i, carry):
            fn(i)
            return carry
        lax.fori_loop(lo, hi, step, 0)

    barrier = pltpu.get_barrier_semaphore()
    for dev in (to_core, to_x, to_xc, to_y):
        pl.semaphore_signal(barrier, inc=1, device_id=dev, device_id_type=MESH)

    @pl.when(above)
    def _():
        pl.semaphore_signal(barrier, inc=1, device_id=(trial + 2, s), device_id_type=MESH)

    @pl.when(below)
    def _():
        pl.semaphore_signal(barrier, inc=1, device_id=(trial - 2, s), device_id_type=MESH)

    @pl.when(inner)
    def _():
        pl.semaphore_wait(barrier, 6)

    @pl.when(jnp.logical_not(inner))
    def _():
        pl.semaphore_wait(barrier, 5)

    loop(0, head, start_own)

    def begin(j):
        for item in first_copies(j):
            item.start()
        local_dy(j).start()
    loop(0, planes, begin)
    loop(0, chunks, lambda n: local_w(n).start())
    for item in low_copies():
        item.start()
    for item in low_local():
        item.start()

    def spread(j):
        over_x, over_core, from_x, _ = later_copies(j)
        dy_arrived(oy, s, j)
        over_x.start()
        over_core.start()
        dy_arrived(y, s_x, j)
        from_x.start()
        forward(1, j)
    loop(0, planes, spread)
    loop(planes, head, lambda n: forward(1, n))

    def spread_far(j):
        dy_arrived(oy, s_x, j)
        later_copies(j)[3].start()
        for hop in range(2, planes - 1):
            forward(hop, j)
        start_own(head + j)
    loop(0, planes, spread_far)

    def rest(n):
        for hop in range(2, planes - 1):
            forward(hop, n)
        start_own(head + n)
    loop(planes, head, rest)

    def settle(j):
        local_dy(j).wait()
        for yy in (y, oy):
            dy_arrived(yy, s_c, j)
            dy_arrived(yy, s_xc, j)
    loop(0, planes, settle)
    low_settle()
    u_out = pltpu.make_async_copy(uv, uall_ref, up_sem.at[2])
    u_out.start()
    vsum[y] = (vparts[0] + vparts[1] + vparts[2] + vparts[3]).astype(vsum.dtype)
    v_copy().start()

    def put_own(at, value):
        upv[y, :, at] = value
    up_product(y, put_own)

    def up_out(k):
        return pltpu.make_async_copy(
            upv.at[k], up_ref.at[:, pl.ds(pl.multiple_of(k * width, width), width)], up_sem.at[k])

    block = min(512, tokens)

    def product(yy, n, i):
        start = pl.multiple_of(i * block, block)
        total = None
        for j in range(planes):
            piece = lax.dot_general(
                dyv[yy, j, pl.ds(start, block), :],
                wv[j, pl.ds(pl.multiple_of(n * wide, wide), wide), :],
                NT, preferred_element_type=jnp.float32)
            total = piece if total is None else total + piece
        return total, pl.ds(start, block)

    def finish(n):
        partial_copy(n).wait_recv()

        def add(i):
            at = pl.ds(pl.multiple_of(i * block, block), block)
            acc[n % 2, at, :] = acc[n % 2, at, :] + prec[n, at, :].astype(jnp.float32)
        loop(0, tokens // block, add)
        out_copy(n).start()

    def compute(n):
        local_w(n).wait()

        @pl.when(jnp.logical_not(inner))
        def _():
            for hop in range(1, planes):
                @pl.when(z + hop < planes)
                def _():
                    w_arrived(z + hop, n)

                @pl.when(z - hop >= 0)
                def _():
                    w_arrived(z - hop, n)

        def other(i):
            value, at = product(oy, n, i)
            part[n, at, :] = value.astype(part.dtype)
        loop(0, tokens // block, other)
        partial_copy(n).start()

        @pl.when(n >= 2)
        def _():
            out_copy(n - 2).wait()

        def own(i):
            value, at = product(y, n, i)
            acc[n % 2, at, :] = value
        loop(0, tokens // block, own)

        @pl.when(n >= 1)
        def _():
            finish(n - 1)

    def early(n):
        forward(1, head + n)
        compute(n)
    loop(0, head, early)

    def late(n):
        for hop in range(2, planes - 1):
            forward(hop, n)
    v_copy().wait_recv()

    def put_given(at, value):
        upg[:, at] = value
    up_product(oy, put_given)
    up_copy().start()
    loop(head, chunks, late)
    up_copy().wait_recv()
    up_out(y).start()
    up_out(oy).start()
    loop(head, chunks, compute)
    finish(chunks - 1)

    out_copy(chunks - 2).wait()
    out_copy(chunks - 1).wait()
    u_out.wait()
    up_out(y).wait()
    up_out(oy).wait()
    for item in low_copies():
        item.wait_send()
    v_copy().wait_send()
    up_copy().wait_send()

    def drain_dy(j):
        for item in first_copies(j) + later_copies(j):
            item.wait_send()
    loop(0, planes, drain_dy)

    def drain(n):
        partial_copy(n).wait_send()

        @pl.when(above)
        def _():
            w_send(z, n, True, True).wait_send()

        @pl.when(below)
        def _():
            w_send(z, n, False, True).wait_send()

        for hop in range(1, planes - 1):
            @pl.when(jnp.logical_and(inner, z + hop < planes))
            def _():
                w_send(z + hop, n, False, False).wait_send()

            @pl.when(jnp.logical_and(inner, z - hop >= 0))
            def _():
                w_send(z - hop, n, True, False).wait_send()
    loop(0, chunks, drain)


def dense_exchange(planes, gradient_rows, weight, u_part, v_partial):
    rows, width = gradient_rows.shape[0], weight.shape[1]
    tokens, heads = rows * 4, weight.shape[0]
    rank = u_part.shape[1]
    wide = min(256, heads // 8)
    chunks = heads // wide
    dma = pltpu.SemaphoreType.DMA
    bf16, f32 = jnp.bfloat16, jnp.float32
    return pl.pallas_call(
        functools.partial(dense_kernel, planes, chunks, wide),
        out_shape=(
            jax.ShapeDtypeStruct((tokens, heads), f32),
            jax.ShapeDtypeStruct((tokens, rank), bf16),
            jax.ShapeDtypeStruct((rank, 2 * width), f32),
        ),
        in_specs=[pl.BlockSpec(memory_space=pl.ANY)] * 4,
        out_specs=[pl.BlockSpec(memory_space=pl.ANY)] * 3,
        scratch_shapes=[
            pltpu.VMEM((planes, heads, width), bf16),
            pltpu.VMEM((2, planes, tokens, width), bf16),
            pltpu.VMEM((chunks, tokens, wide), bf16),
            pltpu.VMEM((chunks, tokens, wide), bf16),
            pltpu.VMEM((2, tokens, wide), f32),
            pltpu.VMEM((tokens, rank), bf16),
            pltpu.VMEM((4, rank, tokens), f32),
            pltpu.VMEM((2, rank, tokens), bf16),
            pltpu.VMEM((2, rank, width), f32),
            pltpu.VMEM((rank, width), f32),
            dma((chunks,)), dma((planes, chunks)), dma((planes, chunks)), dma((planes, chunks)),
            dma((planes,)), dma((planes,)), dma((2, planes)), dma((4, planes)), dma((2, 4, planes)),
            dma((chunks,)), dma((chunks,)), dma((2,)), dma((3,)),
            dma((2,)), dma((2, 3)), dma((4,)), dma((4,)), dma((2,)), dma((2,)),
        ],
        compiler_params=pltpu.CompilerParams(
            collective_id=0, has_side_effects=True, vmem_limit_bytes=60 * 2**20),
        cost_estimate=pl.CostEstimate(
            flops=4 * tokens * heads * planes * width, bytes_accessed=2**27, transcendentals=0),
    )(gradient_rows, weight, u_part, v_partial)


def line_body(
    planes, stored_attention, output_gradient, output_weight, down_adapter, up_adapter, lengths, ranks
):
    attention_rows = stored_attention[0]
    gradient_rows = output_gradient[0]
    down_piece = down_adapter[0]
    up_complete = up_adapter[0]
    adapter_rank = ranks[0]
    token_rows = attention_rows.shape[0]
    rank_mask = jnp.arange(up_complete.shape[0]) < adapter_rank
    adapter_scale = adapter_alpha / jnp.sqrt(adapter_rank.astype(jnp.float32))
    a_low = jnp.where(rank_mask[None, :], down_piece, jnp.zeros_like(down_piece))
    b_low = jnp.where(rank_mask[:, None], up_complete, jnp.zeros_like(up_complete))
    live = jnp.arange(token_rows) < lengths[0]
    shard_rows = gradient_rows.shape[0]
    live_rows = lax.axis_index("tensor") * shard_rows + jnp.arange(shard_rows) < lengths[0]
    u_part = jnp.einsum("td,rd->tr", gradient_rows, b_low, preferred_element_type=jnp.float32)
    u_part = jnp.where(live_rows[:, None], u_part, 0.0).astype(jnp.bfloat16)
    v_partial = jnp.einsum("tk,kr->rt", attention_rows, a_low, preferred_element_type=jnp.float32)
    v_partial = jnp.where(live[None, :], v_partial, 0.0)

    dense, u_all, up_total = dense_exchange(
        planes, gradient_rows, output_weight, u_part, v_partial)

    lowrank_piece = jnp.einsum("tr,hr->th", u_all, a_low, preferred_element_type=jnp.float32)
    attention_gradient = jnp.where(live[:, None], dense + adapter_scale * lowrank_piece, 0.0).astype(jnp.bfloat16)
    down_total = jnp.einsum("th,tr->hr", attention_rows, u_all, preferred_element_type=jnp.float32)
    down_gradient = adapter_scale * down_total / float(token_rows)
    up_gradient = adapter_scale * up_total / float(token_rows)
    return (attention_gradient[None], down_gradient[None], up_gradient[None])


def body(
    stored_attention, output_gradient, output_weight, down_adapter, up_adapter, lengths, ranks
):
    attention_rows = stored_attention[0]
    gradient_rows = output_gradient[0]
    down_piece = down_adapter[0]
    up_complete = up_adapter[0]
    length = lengths[0]
    adapter_rank = ranks[0]
    token_rows = attention_rows.shape[0]
    head_cols = attention_rows.shape[1]
    shard_rows = gradient_rows.shape[0]
    rank_mask = jnp.arange(up_complete.shape[0]) < adapter_rank
    adapter_scale = adapter_alpha / jnp.sqrt(adapter_rank.astype(jnp.float32))
    a_low = jnp.where(rank_mask[None, :], down_piece, jnp.zeros_like(down_piece))
    b_low = jnp.where(rank_mask[:, None], up_complete, jnp.zeros_like(up_complete))
    row_offset = lax.axis_index("tensor") * shard_rows
    live_rows = row_offset + jnp.arange(shard_rows) < length
    gradient_rows = jnp.where(live_rows[:, None], gradient_rows, jnp.zeros_like(gradient_rows))
    u_part = jnp.einsum(
        "td,rd->tr", gradient_rows, b_low, preferred_element_type=jnp.float32
    ).astype(jnp.bfloat16)
    v_partial = jnp.dot(attention_rows, a_low, preferred_element_type=jnp.float32)
    lowrank_right = lax.psum(v_partial, "tensor").astype(jnp.bfloat16)
    col_start = lax.axis_index("tensor") * head_cols
    rows_all, u_all = (
        lax.all_gather(gradient_rows, "tensor", axis=0, tiled=True),
        lax.all_gather(u_part, "tensor", axis=0, tiled=True),
    )
    dense_piece = row_product(rows_all, lax.all_gather(output_weight, "trial", axis=1, tiled=True))
    lowrank_piece = jnp.einsum("tr,hr->th", u_all, a_low, preferred_element_type=jnp.float32)
    attention_gradient = (dense_piece + adapter_scale * lowrank_piece).astype(jnp.bfloat16)
    down_total = jnp.einsum("th,tr->hr", attention_rows, u_all, preferred_element_type=jnp.float32)
    own_cols = lax.dynamic_slice_in_dim(rows_all, col_start, head_cols, 1)
    up_total = jnp.einsum("tr,th->rh", lowrank_right, own_cols, preferred_element_type=jnp.float32)
    down_gradient = adapter_scale * down_total / float(token_rows)
    up_gradient = adapter_scale * up_total / float(token_rows)
    return (attention_gradient[None], down_gradient[None], up_gradient[None])


def solution(mesh):
    placed = (
        P("trial", None, "tensor"),
        P("trial", "tensor", None),
        P("tensor", "trial"),
        P("trial", "tensor", None),
        P("trial", None, None),
        P("trial"),
        P("trial"),
    )
    trials, tensors = mesh.shape["trial"], mesh.shape["tensor"]
    if tensors == 4 and trials == 2 * tensors:
        run = functools.partial(line_body, trials // 2)
    else:
        run = body
    return jax.shard_map(
        run,
        mesh=mesh,
        in_specs=placed,
        out_specs=(
            P("trial", None, "tensor"),
            P("trial", "tensor", None),
            P("trial", None, "tensor"),
        ),
        check_vma=False,
    )
```

```python
import functools

import jax
import jax.numpy as jnp
from jax import lax
from jax.experimental import pallas as pl
from jax.experimental.pallas import tpu as pltpu
from jax.sharding import PartitionSpec as P

adapter_alpha = 32.0
MESH = pl.DeviceIdType.MESH
NT = (((1,), (1,)), ((), ()))


def row_product(left, right):
    return jnp.einsum("tk,hk->th", left, right, preferred_element_type=jnp.float32)


def dense_kernel(
    planes, chunks, wide,
    dy_ref, w_ref, att_ref, a_ref, b_ref, mask_ref, dense_ref, uall_ref, up_ref,
    wv, dyv, part, prec, acc, uv, vparts, vsum, upv, upg, dyo, attv, av, bv,
    w_loc, w_up, w_dn, w_recv,
    dy_loc, dyy_send, dyx_send, dyc_send, dy_recv,
    p_send, p_recv, o_sem, up_sem,
    far_loc, low_loc, low_send, u_recv, v_recv, pair_send, pair_recv,
):
    trial, s = lax.axis_index("trial"), lax.axis_index("tensor")
    z, y = trial // 2, trial % 2
    x, c = s // 2, s % 2
    oy = 1 - y
    s_c, s_x, s_xc = 2 * x + 1 - c, 2 * (1 - x) + c, 2 * (1 - x) + 1 - c
    rows, width = dy_ref.shape[0], w_ref.shape[1]
    tokens = dyv.shape[2]
    head = chunks // 2
    to_core, to_x, to_y = (trial, s_c), (trial, s_x), (2 * z + oy, s)
    to_xc = (trial, s_xc)
    above, below = z < planes - 1, z > 0
    inner = jnp.logical_and(above, below)

    def copy(src, dst, ss, rs, dev):
        return pltpu.make_async_remote_copy(
            src_ref=src, dst_ref=dst, send_sem=ss, recv_sem=rs,
            device_id=dev, device_id_type=MESH)

    def w_slot(zz, n):
        return wv.at[zz, pl.ds(pl.multiple_of(n * wide, wide), wide), :]

    def w_own(n):
        return w_ref.at[pl.ds(pl.multiple_of(n * wide, wide), wide), :]

    def w_send(zz, n, up, own):
        src = w_own(n) if own else w_slot(zz, n)
        sem = w_up if up else w_dn
        dev = (trial + 2, s) if up else (trial - 2, s)
        return copy(src, w_slot(zz, n), sem.at[zz, n], w_recv.at[zz, n], dev)

    def w_arrived(zz, n):
        copy(w_slot(zz, n), w_slot(zz, n), w_up.at[zz, n], w_recv.at[zz, n], to_y).wait_recv()

    def start_own(n):
        @pl.when(above)
        def _():
            w_send(z, n, True, True).start()

        @pl.when(below)
        def _():
            w_send(z, n, False, True).start()

    def forward(hop, n):
        @pl.when(jnp.logical_and(inner, z + hop < planes))
        def _():
            w_arrived(z + hop, n)
            w_send(z + hop, n, False, False).start()

        @pl.when(jnp.logical_and(inner, z - hop >= 0))
        def _():
            w_arrived(z - hop, n)
            w_send(z - hop, n, True, False).start()

    def dy_own(j, parity):
        start = pl.multiple_of((2 * j + parity) * width, width)
        return dy_ref.at[:, pl.ds(start, width)]

    def dy_slot(yy, ss, j):
        return dyv.at[yy, j, pl.ds(pl.multiple_of(ss * rows, rows), rows), :]

    def dy_send(src, yy, ss, j, sem, dev):
        return copy(src, dy_slot(yy, ss, j), sem, dy_recv.at[yy, ss, j], dev)

    def dy_arrived(yy, ss, j):
        slot = dy_slot(yy, ss, j)
        dy_send(slot, yy, ss, j, dyy_send.at[j], to_y).wait_recv()

    def first_copies(j):
        return (
            dy_send(dy_own(j, oy), y, s, j, dyy_send.at[j], to_y),
            dy_send(dy_own(j, y), y, s, j, dyx_send.at[0, j], to_x),
            dy_send(dy_own(j, y), y, s, j, dyc_send.at[0, j], to_core),
        )

    def local_dy(j):
        return pltpu.make_async_copy(dy_own(j, y), dy_slot(y, s, j), dy_loc.at[j])

    def local_w(n):
        return pltpu.make_async_copy(w_own(n), w_slot(z, n), w_loc.at[n])

    def later_copies(j):
        return (
            dy_send(dy_slot(oy, s, j), oy, s, j, dyx_send.at[1, j], to_x),
            dy_send(dy_slot(oy, s, j), oy, s, j, dyc_send.at[1, j], to_core),
            dy_send(dy_slot(y, s_x, j), y, s_x, j, dyc_send.at[2, j], to_core),
            dy_send(dy_slot(oy, s_x, j), oy, s_x, j, dyc_send.at[3, j], to_core),
        )

    block = min(512, tokens)

    def partial_copy(n, i):
        at = pl.ds(pl.multiple_of(i * block, block), block)
        return copy(part.at[n, at, :], prec.at[n, at, :], p_send.at[n, i], p_recv.at[n, i], to_y)

    def out_copy(n):
        cols = pl.ds(pl.multiple_of(n * wide, wide), wide)
        return pltpu.make_async_copy(acc.at[n % 2], dense_ref.at[:, cols], o_sem.at[n % 2])

    def u_slot(ss):
        return uv.at[pl.ds(pl.multiple_of(ss * rows, rows), rows), :]

    peers = ((to_core, s_c), (to_x, s_x), (to_xc, s_xc))

    def low_copies():
        return [
            copy(src, dst, low_send.at[i, k], sem.at[s], dev)
            for k, (dev, _) in enumerate(peers)
            for i, (src, dst, sem) in enumerate(
                ((u_slot(s), u_slot(s), u_recv), (vparts.at[s], vparts.at[s], v_recv)))
        ]

    def low_local():
        return (
            pltpu.make_async_copy(b_ref, bv, low_loc.at[0]),
            pltpu.make_async_copy(att_ref, attv, low_loc.at[1]),
            pltpu.make_async_copy(a_ref, av, low_loc.at[2]),
        )

    def far_dy(j):
        return pltpu.make_async_copy(dy_own(j, oy), dyo.at[j], far_loc.at[j])

    def low_compute():
        for item in low_local():
            item.wait()
        step = min(256, tokens)

        def v_rows(i):
            at = pl.ds(pl.multiple_of(i * step, step), step)
            value = jnp.dot(attv[at, :], av[...], preferred_element_type=jnp.float32)
            vparts[s, :, at] = value.T * mask_ref[:, at]
        loop(0, tokens // step, v_rows)
        total = None
        for j in range(planes):
            local_dy(j).wait()
            far_dy(j).wait()
            mine = dyv[y, j, pl.ds(pl.multiple_of(s * rows, rows), rows), :]
            for value, parity in ((mine, y), (dyo[j], oy)):
                at = pl.ds(pl.multiple_of((2 * j + parity) * width, width), width)
                piece = lax.dot_general(value, bv[:, at], NT, preferred_element_type=jnp.float32)
                total = piece if total is None else total + piece
        uv[pl.ds(pl.multiple_of(s * rows, rows), rows), :] = total.astype(uv.dtype)

    def low_settle():
        for k, (dev, ss) in enumerate(peers):
            copy(u_slot(ss), u_slot(ss), low_send.at[0, k], u_recv.at[ss], dev).wait_recv()
            copy(vparts.at[ss], vparts.at[ss], low_send.at[1, k], v_recv.at[ss], dev).wait_recv()

    def v_copy():
        return copy(vsum.at[y], vsum.at[y], pair_send.at[0], pair_recv.at[0], to_y)

    def up_copy():
        return copy(upg, upv.at[y], pair_send.at[1], pair_recv.at[1], to_y)

    def up_product(yy, put):
        step = min(256, width)
        for i in range(width // step):
            at = pl.ds(i * step, step)
            put(at, jnp.dot(vsum[yy], dyv[yy, s, :, at], preferred_element_type=jnp.float32))

    def loop(lo, hi, fn):
        def step(i, carry):
            fn(i)
            return carry
        lax.fori_loop(lo, hi, step, 0)

    barrier = pltpu.get_barrier_semaphore()
    for dev in (to_core, to_x, to_xc, to_y):
        pl.semaphore_signal(barrier, inc=1, device_id=dev, device_id_type=MESH)

    @pl.when(above)
    def _():
        pl.semaphore_signal(barrier, inc=1, device_id=(trial + 2, s), device_id_type=MESH)

    @pl.when(below)
    def _():
        pl.semaphore_signal(barrier, inc=1, device_id=(trial - 2, s), device_id_type=MESH)

    @pl.when(inner)
    def _():
        pl.semaphore_wait(barrier, 6)

    @pl.when(jnp.logical_not(inner))
    def _():
        pl.semaphore_wait(barrier, 5)

    loop(0, head, start_own)

    def begin(j):
        for item in first_copies(j):
            item.start()
        local_dy(j).start()
    loop(0, planes, begin)
    loop(0, chunks, lambda n: local_w(n).start())
    for item in low_local():
        item.start()
    loop(0, planes, lambda j: far_dy(j).start())
    low_compute()
    for item in low_copies():
        item.start()

    def spread(j):
        over_x, over_core, from_x, _ = later_copies(j)
        dy_arrived(oy, s, j)
        over_x.start()
        over_core.start()
        dy_arrived(y, s_x, j)
        from_x.start()
        forward(1, j)
    loop(0, planes, spread)
    loop(planes, head, lambda n: forward(1, n))

    def spread_far(j):
        dy_arrived(oy, s_x, j)
        later_copies(j)[3].start()
        for hop in range(2, planes - 1):
            forward(hop, j)
        start_own(head + j)
    loop(0, planes, spread_far)

    def rest(n):
        for hop in range(2, planes - 1):
            forward(hop, n)
        start_own(head + n)
    loop(planes, head, rest)

    def settle(j):
        for yy in (y, oy):
            dy_arrived(yy, s_c, j)
            dy_arrived(yy, s_xc, j)
    loop(0, planes, settle)
    low_settle()
    u_out = pltpu.make_async_copy(uv, uall_ref, up_sem.at[2])
    u_out.start()
    vsum[y] = (vparts[0] + vparts[1] + vparts[2] + vparts[3]).astype(vsum.dtype)
    v_copy().start()

    def put_own(at, value):
        upv[y, :, at] = value
    up_product(y, put_own)

    def up_out(k):
        return pltpu.make_async_copy(
            upv.at[k], up_ref.at[:, pl.ds(pl.multiple_of(k * width, width), width)], up_sem.at[k])

    def product(yy, n, i):
        start = pl.multiple_of(i * block, block)
        total = None
        for j in range(planes):
            piece = lax.dot_general(
                dyv[yy, j, pl.ds(start, block), :],
                wv[j, pl.ds(pl.multiple_of(n * wide, wide), wide), :],
                NT, preferred_element_type=jnp.float32)
            total = piece if total is None else total + piece
        return total, pl.ds(start, block)

    def finish(n):
        def add(i):
            partial_copy(n, i).wait_recv()
            at = pl.ds(pl.multiple_of(i * block, block), block)
            acc[n % 2, at, :] = acc[n % 2, at, :] + prec[n, at, :].astype(jnp.float32)
        loop(0, tokens // block, add)
        out_copy(n).start()

    def compute(n):
        local_w(n).wait()

        @pl.when(jnp.logical_not(inner))
        def _():
            for hop in range(1, planes):
                @pl.when(z + hop < planes)
                def _():
                    w_arrived(z + hop, n)

                @pl.when(z - hop >= 0)
                def _():
                    w_arrived(z - hop, n)

        def other(i):
            value, at = product(oy, n, i)
            part[n, at, :] = value.astype(part.dtype)
            partial_copy(n, i).start()
        loop(0, tokens // block, other)

        @pl.when(n >= 2)
        def _():
            out_copy(n - 2).wait()

        def own(i):
            value, at = product(y, n, i)
            acc[n % 2, at, :] = value
        loop(0, tokens // block, own)

        @pl.when(n >= 1)
        def _():
            finish(n - 1)

    def early(n):
        forward(1, head + n)
        compute(n)
    loop(0, head, early)

    def late(n):
        for hop in range(2, planes - 1):
            forward(hop, n)
    v_copy().wait_recv()

    def put_given(at, value):
        upg[:, at] = value
    up_product(oy, put_given)
    up_copy().start()
    loop(head, chunks, late)
    up_copy().wait_recv()
    up_out(y).start()
    up_out(oy).start()
    loop(head, chunks, compute)
    finish(chunks - 1)

    out_copy(chunks - 2).wait()
    out_copy(chunks - 1).wait()
    u_out.wait()
    up_out(y).wait()
    up_out(oy).wait()
    for item in low_copies():
        item.wait_send()
    v_copy().wait_send()
    up_copy().wait_send()

    def drain_dy(j):
        for item in first_copies(j) + later_copies(j):
            item.wait_send()
    loop(0, planes, drain_dy)

    def drain(n):
        loop(0, tokens // block, lambda i: partial_copy(n, i).wait_send())

        @pl.when(above)
        def _():
            w_send(z, n, True, True).wait_send()

        @pl.when(below)
        def _():
            w_send(z, n, False, True).wait_send()

        for hop in range(1, planes - 1):
            @pl.when(jnp.logical_and(inner, z + hop < planes))
            def _():
                w_send(z + hop, n, False, False).wait_send()

            @pl.when(jnp.logical_and(inner, z - hop >= 0))
            def _():
                w_send(z - hop, n, True, False).wait_send()
    loop(0, chunks, drain)


def dense_exchange(planes, gradient_rows, weight, attention, down, up, live):
    rows, width = gradient_rows.shape[0], weight.shape[1]
    tokens, heads = rows * 4, weight.shape[0]
    rank = up.shape[0]
    halves = max(1, tokens // 512)
    any_space, vmem = pl.BlockSpec(memory_space=pl.ANY), pl.BlockSpec(memory_space=pltpu.VMEM)
    wide = min(256, heads // 8)
    chunks = heads // wide
    dma = pltpu.SemaphoreType.DMA
    bf16, f32 = jnp.bfloat16, jnp.float32
    return pl.pallas_call(
        functools.partial(dense_kernel, planes, chunks, wide),
        out_shape=(
            jax.ShapeDtypeStruct((tokens, heads), f32),
            jax.ShapeDtypeStruct((tokens, rank), bf16),
            jax.ShapeDtypeStruct((rank, 2 * width), f32),
        ),
        in_specs=[any_space] * 5 + [vmem],
        out_specs=[any_space] * 3,
        scratch_shapes=[
            pltpu.VMEM((planes, heads, width), bf16),
            pltpu.VMEM((2, planes, tokens, width), bf16),
            pltpu.VMEM((chunks, tokens, wide), bf16),
            pltpu.VMEM((chunks, tokens, wide), bf16),
            pltpu.VMEM((2, tokens, wide), f32),
            pltpu.VMEM((tokens, rank), bf16),
            pltpu.VMEM((4, rank, tokens), f32),
            pltpu.VMEM((2, rank, tokens), bf16),
            pltpu.VMEM((2, rank, width), f32),
            pltpu.VMEM((rank, width), f32),
            pltpu.VMEM((planes, rows, width), bf16),
            pltpu.VMEM(attention.shape, bf16),
            pltpu.VMEM(down.shape, bf16),
            pltpu.VMEM(up.shape, bf16),
            dma((chunks,)), dma((planes, chunks)), dma((planes, chunks)), dma((planes, chunks)),
            dma((planes,)), dma((planes,)), dma((2, planes)), dma((4, planes)), dma((2, 4, planes)),
            dma((chunks, halves)), dma((chunks, halves)), dma((2,)), dma((3,)),
            dma((planes,)), dma((3,)), dma((2, 3)), dma((4,)), dma((4,)), dma((2,)), dma((2,)),
        ],
        compiler_params=pltpu.CompilerParams(
            collective_id=0, has_side_effects=True, vmem_limit_bytes=60 * 2**20),
        cost_estimate=pl.CostEstimate(
            flops=4 * tokens * heads * planes * width, bytes_accessed=2**27, transcendentals=0),
    )(gradient_rows, weight, attention, down, up, live)


def line_body(
    planes, stored_attention, output_gradient, output_weight, down_adapter, up_adapter, lengths, ranks
):
    attention_rows = stored_attention[0]
    gradient_rows = output_gradient[0]
    down_piece = down_adapter[0]
    up_complete = up_adapter[0]
    adapter_rank = ranks[0]
    token_rows = attention_rows.shape[0]
    rank_mask = jnp.arange(up_complete.shape[0]) < adapter_rank
    adapter_scale = adapter_alpha / jnp.sqrt(adapter_rank.astype(jnp.float32))
    a_low = jnp.where(rank_mask[None, :], down_piece, jnp.zeros_like(down_piece))
    live = jnp.arange(token_rows) < lengths[0]
    dense, u_all, up_total = dense_exchange(
        planes, gradient_rows, output_weight, attention_rows, down_piece, up_complete,
        live.astype(jnp.float32)[None, :])
    u_all = jnp.where(live[:, None] & rank_mask[None, :], u_all, jnp.zeros_like(u_all))
    up_total = jnp.where(rank_mask[:, None], up_total, 0.0)

    lowrank_piece = jnp.einsum("tr,hr->th", u_all, a_low, preferred_element_type=jnp.float32)
    attention_gradient = jnp.where(live[:, None], dense + adapter_scale * lowrank_piece, 0.0).astype(jnp.bfloat16)
    down_total = jnp.einsum("th,tr->hr", attention_rows, u_all, preferred_element_type=jnp.float32)
    down_gradient = adapter_scale * down_total / float(token_rows)
    up_gradient = adapter_scale * up_total / float(token_rows)
    return (attention_gradient[None], down_gradient[None], up_gradient[None])


def body(
    stored_attention, output_gradient, output_weight, down_adapter, up_adapter, lengths, ranks
):
    attention_rows = stored_attention[0]
    gradient_rows = output_gradient[0]
    down_piece = down_adapter[0]
    up_complete = up_adapter[0]
    length = lengths[0]
    adapter_rank = ranks[0]
    token_rows = attention_rows.shape[0]
    head_cols = attention_rows.shape[1]
    shard_rows = gradient_rows.shape[0]
    rank_mask = jnp.arange(up_complete.shape[0]) < adapter_rank
    adapter_scale = adapter_alpha / jnp.sqrt(adapter_rank.astype(jnp.float32))
    a_low = jnp.where(rank_mask[None, :], down_piece, jnp.zeros_like(down_piece))
    b_low = jnp.where(rank_mask[:, None], up_complete, jnp.zeros_like(up_complete))
    row_offset = lax.axis_index("tensor") * shard_rows
    live_rows = row_offset + jnp.arange(shard_rows) < length
    gradient_rows = jnp.where(live_rows[:, None], gradient_rows, jnp.zeros_like(gradient_rows))
    u_part = jnp.einsum(
        "td,rd->tr", gradient_rows, b_low, preferred_element_type=jnp.float32
    ).astype(jnp.bfloat16)
    v_partial = jnp.dot(attention_rows, a_low, preferred_element_type=jnp.float32)
    lowrank_right = lax.psum(v_partial, "tensor").astype(jnp.bfloat16)
    col_start = lax.axis_index("tensor") * head_cols
    rows_all, u_all = (
        lax.all_gather(gradient_rows, "tensor", axis=0, tiled=True),
        lax.all_gather(u_part, "tensor", axis=0, tiled=True),
    )
    dense_piece = row_product(rows_all, lax.all_gather(output_weight, "trial", axis=1, tiled=True))
    lowrank_piece = jnp.einsum("tr,hr->th", u_all, a_low, preferred_element_type=jnp.float32)
    attention_gradient = (dense_piece + adapter_scale * lowrank_piece).astype(jnp.bfloat16)
    down_total = jnp.einsum("th,tr->hr", attention_rows, u_all, preferred_element_type=jnp.float32)
    own_cols = lax.dynamic_slice_in_dim(rows_all, col_start, head_cols, 1)
    up_total = jnp.einsum("tr,th->rh", lowrank_right, own_cols, preferred_element_type=jnp.float32)
    down_gradient = adapter_scale * down_total / float(token_rows)
    up_gradient = adapter_scale * up_total / float(token_rows)
    return (attention_gradient[None], down_gradient[None], up_gradient[None])


def solution(mesh):
    placed = (
        P("trial", None, "tensor"),
        P("trial", "tensor", None),
        P("tensor", "trial"),
        P("trial", "tensor", None),
        P("trial", None, None),
        P("trial"),
        P("trial"),
    )
    trials, tensors = mesh.shape["trial"], mesh.shape["tensor"]
    if tensors == 4 and trials == 2 * tensors:
        run = functools.partial(line_body, trials // 2)
    else:
        run = body
    return jax.shard_map(
        run,
        mesh=mesh,
        in_specs=placed,
        out_specs=(
            P("trial", None, "tensor"),
            P("trial", "tensor", None),
            P("trial", None, "tensor"),
        ),
        check_vma=False,
    )
```

```python
import functools

import jax
import jax.numpy as jnp
from jax import lax
from jax.experimental import pallas as pl
from jax.experimental.pallas import tpu as pltpu
from jax.sharding import PartitionSpec as P

adapter_alpha = 32.0
MESH = pl.DeviceIdType.MESH
NT = (((1,), (1,)), ((), ()))


def row_product(left, right):
    return jnp.einsum("tk,hk->th", left, right, preferred_element_type=jnp.float32)


def dense_kernel(
    planes, chunks, wide,
    dy_ref, w_ref, att_ref, a_ref, b_ref, mask_ref, dense_ref, uall_ref, up_ref,
    wv, dyv, part, prec, acc, uv, vparts, vsum, upv, upg, dyo, attv, av, bv,
    w_loc, w_up, w_dn, w_recv,
    dy_loc, dyy_send, dyx_send, dyc_send, dy_recv,
    p_send, p_recv, o_sem, up_sem,
    far_loc, low_loc, low_send, u_recv, v_recv, pair_send, pair_recv,
):
    trial, s = lax.axis_index("trial"), lax.axis_index("tensor")
    z, y = trial // 2, trial % 2
    x, c = s // 2, s % 2
    oy = 1 - y
    s_c, s_x, s_xc = 2 * x + 1 - c, 2 * (1 - x) + c, 2 * (1 - x) + 1 - c
    rows, width = dy_ref.shape[0], w_ref.shape[1]
    tokens = dyv.shape[2]
    head = chunks // 2
    to_core, to_x, to_y = (trial, s_c), (trial, s_x), (2 * z + oy, s)
    to_xc = (trial, s_xc)
    above, below = z < planes - 1, z > 0
    inner = jnp.logical_and(above, below)

    def copy(src, dst, ss, rs, dev):
        return pltpu.make_async_remote_copy(
            src_ref=src, dst_ref=dst, send_sem=ss, recv_sem=rs,
            device_id=dev, device_id_type=MESH)

    def w_slot(zz, n):
        return wv.at[zz, pl.ds(pl.multiple_of(n * wide, wide), wide), :]

    def w_own(n):
        return w_ref.at[pl.ds(pl.multiple_of(n * wide, wide), wide), :]

    def w_send(zz, n, up, own):
        src = w_own(n) if own else w_slot(zz, n)
        sem = w_up if up else w_dn
        dev = (trial + 2, s) if up else (trial - 2, s)
        return copy(src, w_slot(zz, n), sem.at[zz, n], w_recv.at[zz, n], dev)

    def w_arrived(zz, n):
        copy(w_slot(zz, n), w_slot(zz, n), w_up.at[zz, n], w_recv.at[zz, n], to_y).wait_recv()

    def start_own(n):
        @pl.when(above)
        def _():
            w_send(z, n, True, True).start()

        @pl.when(below)
        def _():
            w_send(z, n, False, True).start()

    def forward(hop, n):
        @pl.when(jnp.logical_and(inner, z + hop < planes))
        def _():
            w_arrived(z + hop, n)
            w_send(z + hop, n, False, False).start()

        @pl.when(jnp.logical_and(inner, z - hop >= 0))
        def _():
            w_arrived(z - hop, n)
            w_send(z - hop, n, True, False).start()

    def dy_own(j, parity):
        start = pl.multiple_of((2 * j + parity) * width, width)
        return dy_ref.at[:, pl.ds(start, width)]

    def dy_slot(yy, ss, j):
        return dyv.at[yy, j, pl.ds(pl.multiple_of(ss * rows, rows), rows), :]

    def dy_send(src, yy, ss, j, sem, dev):
        return copy(src, dy_slot(yy, ss, j), sem, dy_recv.at[yy, ss, j], dev)

    def dy_arrived(yy, ss, j):
        slot = dy_slot(yy, ss, j)
        dy_send(slot, yy, ss, j, dyy_send.at[j], to_y).wait_recv()

    def first_copies(j):
        return (
            dy_send(dy_own(j, oy), y, s, j, dyy_send.at[j], to_y),
            dy_send(dy_own(j, y), y, s, j, dyx_send.at[0, j], to_x),
            dy_send(dy_own(j, y), y, s, j, dyc_send.at[0, j], to_core),
        )

    def local_dy(j):
        return pltpu.make_async_copy(dy_own(j, y), dy_slot(y, s, j), dy_loc.at[j])

    def local_w(n):
        return pltpu.make_async_copy(w_own(n), w_slot(z, n), w_loc.at[n])

    def later_copies(j):
        return (
            dy_send(dy_slot(oy, s, j), oy, s, j, dyx_send.at[1, j], to_x),
            dy_send(dy_slot(oy, s, j), oy, s, j, dyc_send.at[1, j], to_core),
            dy_send(dy_slot(y, s_x, j), y, s_x, j, dyc_send.at[2, j], to_core),
            dy_send(dy_slot(oy, s_x, j), oy, s_x, j, dyc_send.at[3, j], to_core),
        )

    block = min(512, tokens)

    def partial_copy(n, i):
        at = pl.ds(pl.multiple_of(i * block, block), block)
        return copy(part.at[n, at, :], prec.at[n, at, :], p_send.at[n, i], p_recv.at[n, i], to_y)

    def out_copy(n):
        cols = pl.ds(pl.multiple_of(n * wide, wide), wide)
        return pltpu.make_async_copy(acc.at[n % 2], dense_ref.at[:, cols], o_sem.at[n % 2])

    def u_slot(ss):
        return uv.at[pl.ds(pl.multiple_of(ss * rows, rows), rows), :]

    peers = ((to_core, s_c), (to_x, s_x), (to_xc, s_xc))

    def low_copies():
        return [
            copy(src, dst, low_send.at[i, k], sem.at[s], dev)
            for k, (dev, _) in enumerate(peers)
            for i, (src, dst, sem) in enumerate(
                ((u_slot(s), u_slot(s), u_recv), (vparts.at[s], vparts.at[s], v_recv)))
        ]

    def low_local():
        return (
            pltpu.make_async_copy(b_ref, bv, low_loc.at[0]),
            pltpu.make_async_copy(att_ref, attv, low_loc.at[1]),
            pltpu.make_async_copy(a_ref, av, low_loc.at[2]),
        )

    def far_dy(j):
        return pltpu.make_async_copy(dy_own(j, oy), dyo.at[j], far_loc.at[j])

    def low_compute():
        for item in low_local():
            item.wait()
        step = min(256, tokens)

        def v_rows(i):
            at = pl.ds(pl.multiple_of(i * step, step), step)
            value = jnp.dot(attv[at, :], av[...], preferred_element_type=jnp.float32)
            vparts[s, :, at] = value.T * mask_ref[:, at]
        loop(0, tokens // step, v_rows)
        total = None
        for j in range(planes):
            local_dy(j).wait()
            far_dy(j).wait()
            mine = dyv[y, j, pl.ds(pl.multiple_of(s * rows, rows), rows), :]
            for value, parity in ((mine, y), (dyo[j], oy)):
                at = pl.ds(pl.multiple_of((2 * j + parity) * width, width), width)
                piece = lax.dot_general(value, bv[:, at], NT, preferred_element_type=jnp.float32)
                total = piece if total is None else total + piece
        uv[pl.ds(pl.multiple_of(s * rows, rows), rows), :] = total.astype(uv.dtype)

    def low_settle():
        for k, (dev, ss) in enumerate(peers):
            copy(u_slot(ss), u_slot(ss), low_send.at[0, k], u_recv.at[ss], dev).wait_recv()
            copy(vparts.at[ss], vparts.at[ss], low_send.at[1, k], v_recv.at[ss], dev).wait_recv()

    def v_copy():
        return copy(vsum.at[y], vsum.at[y], pair_send.at[0], pair_recv.at[0], to_y)

    def up_copy():
        return copy(upg, upv.at[y], pair_send.at[1], pair_recv.at[1], to_y)

    def up_product(yy, put):
        step = min(256, width)
        for i in range(width // step):
            at = pl.ds(i * step, step)
            put(at, jnp.dot(vsum[yy], dyv[yy, s, :, at], preferred_element_type=jnp.float32))

    def loop(lo, hi, fn):
        def step(i, carry):
            fn(i)
            return carry
        lax.fori_loop(lo, hi, step, 0)

    barrier = pltpu.get_barrier_semaphore()
    for dev in (to_core, to_x, to_xc, to_y):
        pl.semaphore_signal(barrier, inc=1, device_id=dev, device_id_type=MESH)

    @pl.when(above)
    def _():
        pl.semaphore_signal(barrier, inc=1, device_id=(trial + 2, s), device_id_type=MESH)

    @pl.when(below)
    def _():
        pl.semaphore_signal(barrier, inc=1, device_id=(trial - 2, s), device_id_type=MESH)

    @pl.when(inner)
    def _():
        pl.semaphore_wait(barrier, 6)

    @pl.when(jnp.logical_not(inner))
    def _():
        pl.semaphore_wait(barrier, 5)

    loop(0, head, start_own)

    def begin(j):
        for item in first_copies(j):
            item.start()
        local_dy(j).start()
    loop(0, planes, begin)
    loop(0, chunks, lambda n: local_w(n).start())
    for item in low_local():
        item.start()
    loop(0, planes, lambda j: far_dy(j).start())
    low_compute()
    for item in low_copies():
        item.start()

    def spread(j):
        over_x, over_core, from_x, _ = later_copies(j)
        dy_arrived(oy, s, j)
        over_x.start()
        over_core.start()
        dy_arrived(y, s_x, j)
        from_x.start()
        forward(1, j)
    loop(0, planes, spread)
    loop(planes, head, lambda n: forward(1, n))

    def spread_far(j):
        dy_arrived(oy, s_x, j)
        later_copies(j)[3].start()
        for hop in range(2, planes - 1):
            forward(hop, j)
        start_own(head + j)
    loop(0, planes, spread_far)

    def rest(n):
        for hop in range(2, planes - 1):
            forward(hop, n)
        start_own(head + n)
    loop(planes, head, rest)

    def settle(j):
        for yy in (y, oy):
            dy_arrived(yy, s_c, j)
            dy_arrived(yy, s_xc, j)
    loop(0, planes, settle)
    low_settle()
    u_out = pltpu.make_async_copy(uv, uall_ref, up_sem.at[2])
    u_out.start()
    vsum[y] = (vparts[0] + vparts[1] + vparts[2] + vparts[3]).astype(vsum.dtype)
    v_copy().start()

    def put_own(at, value):
        upv[y, :, at] = value
    up_product(y, put_own)

    def up_out(k):
        return pltpu.make_async_copy(
            upv.at[k], up_ref.at[:, pl.ds(pl.multiple_of(k * width, width), width)], up_sem.at[k])

    def product(yy, n, i):
        start = pl.multiple_of(i * block, block)
        total = None
        for j in range(planes):
            piece = lax.dot_general(
                dyv[yy, j, pl.ds(start, block), :],
                wv[j, pl.ds(pl.multiple_of(n * wide, wide), wide), :],
                NT, preferred_element_type=jnp.float32)
            total = piece if total is None else total + piece
        return total, pl.ds(start, block)

    def finish(n):
        def add(i):
            partial_copy(n, i).wait_recv()
            at = pl.ds(pl.multiple_of(i * block, block), block)
            acc[n % 2, at, :] = acc[n % 2, at, :] + prec[n, at, :].astype(jnp.float32)
        loop(0, tokens // block, add)
        out_copy(n).start()

    def compute(n):
        local_w(n).wait()

        @pl.when(jnp.logical_not(inner))
        def _():
            for hop in range(1, planes):
                @pl.when(z + hop < planes)
                def _():
                    w_arrived(z + hop, n)

                @pl.when(z - hop >= 0)
                def _():
                    w_arrived(z - hop, n)

        def other(i):
            value, at = product(oy, n, i)
            part[n, at, :] = value.astype(part.dtype)
            partial_copy(n, i).start()
        loop(0, tokens // block, other)

        @pl.when(n >= 2)
        def _():
            out_copy(n - 2).wait()

        def own(i):
            value, at = product(y, n, i)
            acc[n % 2, at, :] = value
        loop(0, tokens // block, own)

        @pl.when(n >= 1)
        def _():
            finish(n - 1)

    def early(n):
        forward(1, head + n)
        compute(n)
    loop(0, head, early)

    def late(n):
        for hop in range(2, planes - 1):
            forward(hop, n)
    v_copy().wait_recv()

    def put_given(at, value):
        upg[:, at] = value
    up_product(oy, put_given)
    up_copy().start()
    loop(head, chunks, late)
    up_copy().wait_recv()
    up_out(y).start()
    up_out(oy).start()
    loop(head, chunks, compute)
    finish(chunks - 1)

    out_copy(chunks - 2).wait()
    out_copy(chunks - 1).wait()
    u_out.wait()
    up_out(y).wait()
    up_out(oy).wait()
    for item in low_copies():
        item.wait_send()
    v_copy().wait_send()
    up_copy().wait_send()

    def drain_dy(j):
        for item in first_copies(j) + later_copies(j):
            item.wait_send()
    loop(0, planes, drain_dy)

    def drain(n):
        loop(0, tokens // block, lambda i: partial_copy(n, i).wait_send())

        @pl.when(above)
        def _():
            w_send(z, n, True, True).wait_send()

        @pl.when(below)
        def _():
            w_send(z, n, False, True).wait_send()

        for hop in range(1, planes - 1):
            @pl.when(jnp.logical_and(inner, z + hop < planes))
            def _():
                w_send(z + hop, n, False, False).wait_send()

            @pl.when(jnp.logical_and(inner, z - hop >= 0))
            def _():
                w_send(z - hop, n, True, False).wait_send()
    loop(0, chunks, drain)


def dense_exchange(planes, gradient_rows, weight, attention, down, up, live):
    rows, width = gradient_rows.shape[0], weight.shape[1]
    tokens, heads = rows * 4, weight.shape[0]
    rank = up.shape[0]
    halves = max(1, tokens // 512)
    any_space, vmem = pl.BlockSpec(memory_space=pl.ANY), pl.BlockSpec(memory_space=pltpu.VMEM)
    wide = min(128, heads // 8)
    chunks = heads // wide
    dma = pltpu.SemaphoreType.DMA
    bf16, f32 = jnp.bfloat16, jnp.float32
    return pl.pallas_call(
        functools.partial(dense_kernel, planes, chunks, wide),
        out_shape=(
            jax.ShapeDtypeStruct((tokens, heads), f32),
            jax.ShapeDtypeStruct((tokens, rank), bf16),
            jax.ShapeDtypeStruct((rank, 2 * width), f32),
        ),
        in_specs=[any_space] * 5 + [vmem],
        out_specs=[any_space] * 3,
        scratch_shapes=[
            pltpu.VMEM((planes, heads, width), bf16),
            pltpu.VMEM((2, planes, tokens, width), bf16),
            pltpu.VMEM((chunks, tokens, wide), bf16),
            pltpu.VMEM((chunks, tokens, wide), bf16),
            pltpu.VMEM((2, tokens, wide), f32),
            pltpu.VMEM((tokens, rank), bf16),
            pltpu.VMEM((4, rank, tokens), f32),
            pltpu.VMEM((2, rank, tokens), bf16),
            pltpu.VMEM((2, rank, width), f32),
            pltpu.VMEM((rank, width), f32),
            pltpu.VMEM((planes, rows, width), bf16),
            pltpu.VMEM(attention.shape, bf16),
            pltpu.VMEM(down.shape, bf16),
            pltpu.VMEM(up.shape, bf16),
            dma((chunks,)), dma((planes, chunks)), dma((planes, chunks)), dma((planes, chunks)),
            dma((planes,)), dma((planes,)), dma((2, planes)), dma((4, planes)), dma((2, 4, planes)),
            dma((chunks, halves)), dma((chunks, halves)), dma((2,)), dma((3,)),
            dma((planes,)), dma((3,)), dma((2, 3)), dma((4,)), dma((4,)), dma((2,)), dma((2,)),
        ],
        compiler_params=pltpu.CompilerParams(
            collective_id=0, has_side_effects=True, vmem_limit_bytes=60 * 2**20),
        cost_estimate=pl.CostEstimate(
            flops=4 * tokens * heads * planes * width, bytes_accessed=2**27, transcendentals=0),
    )(gradient_rows, weight, attention, down, up, live)


def line_body(
    planes, stored_attention, output_gradient, output_weight, down_adapter, up_adapter, lengths, ranks
):
    attention_rows = stored_attention[0]
    gradient_rows = output_gradient[0]
    down_piece = down_adapter[0]
    up_complete = up_adapter[0]
    adapter_rank = ranks[0]
    token_rows = attention_rows.shape[0]
    rank_mask = jnp.arange(up_complete.shape[0]) < adapter_rank
    adapter_scale = adapter_alpha / jnp.sqrt(adapter_rank.astype(jnp.float32))
    a_low = jnp.where(rank_mask[None, :], down_piece, jnp.zeros_like(down_piece))
    live = jnp.arange(token_rows) < lengths[0]
    dense, u_all, up_total = dense_exchange(
        planes, gradient_rows, output_weight, attention_rows, down_piece, up_complete,
        live.astype(jnp.float32)[None, :])
    u_all = jnp.where(live[:, None] & rank_mask[None, :], u_all, jnp.zeros_like(u_all))
    up_total = jnp.where(rank_mask[:, None], up_total, 0.0)

    lowrank_piece = jnp.einsum("tr,hr->th", u_all, a_low, preferred_element_type=jnp.float32)
    attention_gradient = jnp.where(live[:, None], dense + adapter_scale * lowrank_piece, 0.0).astype(jnp.bfloat16)
    down_total = jnp.einsum("th,tr->hr", attention_rows, u_all, preferred_element_type=jnp.float32)
    down_gradient = adapter_scale * down_total / float(token_rows)
    up_gradient = adapter_scale * up_total / float(token_rows)
    return (attention_gradient[None], down_gradient[None], up_gradient[None])


def body(
    stored_attention, output_gradient, output_weight, down_adapter, up_adapter, lengths, ranks
):
    attention_rows = stored_attention[0]
    gradient_rows = output_gradient[0]
    down_piece = down_adapter[0]
    up_complete = up_adapter[0]
    length = lengths[0]
    adapter_rank = ranks[0]
    token_rows = attention_rows.shape[0]
    head_cols = attention_rows.shape[1]
    shard_rows = gradient_rows.shape[0]
    rank_mask = jnp.arange(up_complete.shape[0]) < adapter_rank
    adapter_scale = adapter_alpha / jnp.sqrt(adapter_rank.astype(jnp.float32))
    a_low = jnp.where(rank_mask[None, :], down_piece, jnp.zeros_like(down_piece))
    b_low = jnp.where(rank_mask[:, None], up_complete, jnp.zeros_like(up_complete))
    row_offset = lax.axis_index("tensor") * shard_rows
    live_rows = row_offset + jnp.arange(shard_rows) < length
    gradient_rows = jnp.where(live_rows[:, None], gradient_rows, jnp.zeros_like(gradient_rows))
    u_part = jnp.einsum(
        "td,rd->tr", gradient_rows, b_low, preferred_element_type=jnp.float32
    ).astype(jnp.bfloat16)
    v_partial = jnp.dot(attention_rows, a_low, preferred_element_type=jnp.float32)
    lowrank_right = lax.psum(v_partial, "tensor").astype(jnp.bfloat16)
    col_start = lax.axis_index("tensor") * head_cols
    rows_all, u_all = (
        lax.all_gather(gradient_rows, "tensor", axis=0, tiled=True),
        lax.all_gather(u_part, "tensor", axis=0, tiled=True),
    )
    dense_piece = row_product(rows_all, lax.all_gather(output_weight, "trial", axis=1, tiled=True))
    lowrank_piece = jnp.einsum("tr,hr->th", u_all, a_low, preferred_element_type=jnp.float32)
    attention_gradient = (dense_piece + adapter_scale * lowrank_piece).astype(jnp.bfloat16)
    down_total = jnp.einsum("th,tr->hr", attention_rows, u_all, preferred_element_type=jnp.float32)
    own_cols = lax.dynamic_slice_in_dim(rows_all, col_start, head_cols, 1)
    up_total = jnp.einsum("tr,th->rh", lowrank_right, own_cols, preferred_element_type=jnp.float32)
    down_gradient = adapter_scale * down_total / float(token_rows)
    up_gradient = adapter_scale * up_total / float(token_rows)
    return (attention_gradient[None], down_gradient[None], up_gradient[None])


def solution(mesh):
    placed = (
        P("trial", None, "tensor"),
        P("trial", "tensor", None),
        P("tensor", "trial"),
        P("trial", "tensor", None),
        P("trial", None, None),
        P("trial"),
        P("trial"),
    )
    trials, tensors = mesh.shape["trial"], mesh.shape["tensor"]
    if tensors == 4 and trials == 2 * tensors:
        run = functools.partial(line_body, trials // 2)
    else:
        run = body
    return jax.shard_map(
        run,
        mesh=mesh,
        in_specs=placed,
        out_specs=(
            P("trial", None, "tensor"),
            P("trial", "tensor", None),
            P("trial", None, "tensor"),
        ),
        check_vma=False,
    )
```
